32 devices in a mesh: gx: 8 (over y, x, core), gy: 4 (over z).
Axes of the slice: x: 2, y: 2, z: 4, core: 2. Of those that a mesh axis runs over, the one named last changes fastest.
Arguments:
- scalar: float32 [512, 256, 512], P('gx', 'gy'), may hold values from -6 to 6
- prefactor: float32 [512, 256, 512], P('gx', 'gy'), may hold values from 0.05 to 1
- factor_x: float32 [512, 512], P('gx'), may hold values from -0.375 to 0.375
- factor_y: float32 [256, 64], P('gy'), may hold values from -0.5 to 0.5
- factor_z: bfloat16 [512, 128], replicated, may hold values from -0.25 to 0.25
Outputs:
- advanced: float32 [512, 256, 512], P('gx', 'gy')
- core: float32 [512, 64, 128], P('gx', 'gy')
The draws below stay inside these ranges and needn't reach their ends.
All inputs are finite; a program needn't handle non-finite values.
Results may differ from the reference program's by a relative error of at most 0.0029.
Values sent between devices are 32-bit elements; how exact they have to be, the bound alone decides.
No kernel may reach another device: no remote copies, remote signals or barrier semaphores. Data moves between devices by JAX's collectives and lax.ppermute only.
A program may use at most 128 MiB of HBM per device.

```python
import math
import jax
import jax.numpy as jnp
from jax import lax

NZ = 512
RX = 512
RY = 64
RZ = 128
NX = 512
NY = 256


def raised(entries, key, source, target, parts, factor):
    def block_of(axis_at):
        return (jnp.arange(entries.shape[axis_at]) // (entries.shape[axis_at] // parts)).reshape((-1,) + (1,) * (entries.ndim - 1 - axis_at))

    near = jax.random.permutation(key, parts)[block_of(target)]
    other_side = (block_of(target) + parts // 2) % parts
    return jnp.where((block_of(source) == near) | (block_of(source) == other_side), factor * entries, entries)


def steps_of(rng, dims, cuts, smallest, top_value):
    def one(axis_at, blocks):
        steps = jax.random.uniform(jax.random.fold_in(jax.random.fold_in(rng, 6), axis_at), (blocks,), jnp.float32, smallest / len(cuts), top_value / len(cuts))
        return jnp.repeat(jnp.exp(steps), dims[axis_at] // blocks).reshape((-1,) + (1,) * (len(dims) - axis_at - 1))

    gain = one(*cuts[0])
    for cut in cuts[1:]:
        gain = gain * one(*cut)
    return gain


def normal_values(key, extent, scale, limit, pieces=(), kind=jnp.bfloat16):
    factor_of = steps_of(key, extent, pieces, -0.22, 0.18) if pieces else 1.0
    entries = jax.random.normal(key, extent, jnp.float32) * scale * factor_of
    return jnp.minimum(jnp.maximum(entries, -limit), limit).astype(kind)


def bell_draw_with(own_key, extent, deviation, reach, shards, heavy, kind=jnp.bfloat16):
    entries = deviation * jax.random.normal(own_key, extent, jnp.float32)
    if shards:
        entries = entries * steps_of(own_key, extent, shards, -0.22, 0.18)
    return jnp.clip(raised(entries, jax.random.fold_in(own_key, 3), *heavy), -reach, reach).astype(kind)


def setup_inputs(seed: int = 0) -> dict:
    splits = jax.random.split(jax.random.key(seed), 6)
    scalar = normal_values(splits[0], (NX, NY, NZ), 1.0, 6.0, ((0, 8), (1, 4)), jnp.float32)
    prefactor = jnp.clip(jnp.exp(math.log(1.0) - 2.9957323 * jax.random.uniform(splits[1], (NX, NY, NZ), jnp.float32) ** steps_of(splits[1], (NX, NY, NZ), ((0, 8), (1, 4)), -0.2, 0.2)), 0.05, 1.0)
    factor_x = bell_draw_with(splits[2], (NX, RX), NX ** -0.5, 0.375, ((0, 8),), (0, 1, 8, 2.0), jnp.float32)
    factor_y = bell_draw_with(splits[3], (NY, RY), NY ** -0.5, 0.5, ((0, 4),), (0, 1, 4, 2.0), jnp.float32)
    factor_z = normal_values(splits[4], (NZ, RZ), NZ ** -0.5, 0.25)
    return dict(scalar=scalar, prefactor=prefactor, factor_x=factor_x, factor_y=factor_y, factor_z=factor_z)


spread_rate = 0.12
activation = 2.0


def laplace(padded):
    center = padded[1:-1, 1:-1]
    z_padded = jnp.pad(center, ((0, 0), (0, 0), (1, 1)))
    beside = padded[2:, 1:-1] + padded[:-2, 1:-1] + padded[1:-1, 2:] + padded[1:-1, :-2]
    beside = beside + z_padded[:, :, 2:] + z_padded[:, :, :-2]
    return beside - 6.0 * center


def sources(field, prefactor):
    return prefactor * jnp.exp(-activation / (1.0 + field * field))


def rate(field, prefactor):
    padded = jnp.pad(field, ((1, 1), (1, 1), (0, 0)))
    return spread_rate * laplace(padded) + sources(field, prefactor)


def reference(scalar, prefactor, factor_x, factor_y, factor_z):
    first = rate(scalar, prefactor)
    middle = scalar + first
    second = rate(middle, prefactor)
    advanced = scalar + 0.5 * (first + second)
    lowered = lax.optimization_barrier(advanced.astype(jnp.bfloat16)).astype(jnp.float32)
    z_reduced = jnp.dot(lowered.reshape(NX * NY, NZ), factor_z.astype(jnp.float32),
                        precision=lax.Precision.HIGHEST).reshape(NX, NY, RZ)
    y_reduced = jnp.einsum("xyc,yb->xbc", z_reduced, factor_y, precision=lax.Precision.HIGHEST)
    core = jnp.einsum("xa,xbc->abc", factor_x, y_reduced, precision=lax.Precision.HIGHEST)
    return advanced, core
```

```python
import functools
import math

import jax
import jax.numpy as jnp
from jax import lax
from jax.experimental import pallas as pl
from jax.experimental.pallas import tpu as pltpu
from jax.sharding import PartitionSpec as P

spread_rate = 0.12
activation = 2.0
exponent = -activation * math.log2(math.e)
lanes = 128
pad = 8
chunks = 4
f32, bf16 = jnp.float32, jnp.bfloat16
anywhere = pl.BlockSpec(memory_space=pltpu.HBM)
in_vmem = pl.BlockSpec(memory_space=pltpu.VMEM)


def source(field, prefactor):
    return prefactor * jnp.exp2(exponent / (1.0 + field * field))


def along_z(tiles):
    lane = lax.broadcasted_iota(jnp.int32, tiles[0].shape, 1)
    last = len(tiles) - 1
    sums = []
    for k, tile in enumerate(tiles):
        below = tiles[k - 1] if k else 0.0
        above = tiles[k + 1] if k < last else 0.0
        left = pltpu.roll(jnp.where(lane == lanes - 1, below, tile), 1, 1)
        right = pltpu.roll(jnp.where(lane == 0, above, tile), lanes - 1, 1)
        sums.append(left + right)
    return sums


def column(k):
    return slice(k * lanes, (k + 1) * lanes)


def faces_kernel(scalar, prefactor, x_lo, x_hi, y_lo, y_hi, s_rows, p_rows, s_cols, p_cols, line, sems):
    cells_x, cells_y, depth = scalar.shape
    copies = [
        (scalar.at[pl.ds(0, 2)], s_rows.at[0]),
        (scalar.at[pl.ds(cells_x - 2, 2)], s_rows.at[1]),
        (prefactor.at[pl.ds(0, 1)], p_rows.at[0]),
        (prefactor.at[pl.ds(cells_x - 1, 1)], p_rows.at[1]),
        (scalar.at[:, pl.ds(0, 8)], s_cols.at[0]),
        (prefactor.at[:, pl.ds(0, 8)], p_cols.at[0]),
        (scalar.at[:, pl.ds(cells_y - 8, 8)], s_cols.at[1]),
        (prefactor.at[:, pl.ds(cells_y - 8, 8)], p_cols.at[1]),
    ]
    copies = [pltpu.make_async_copy(a, b, sems.at[n]) for n, (a, b) in enumerate(copies)]
    for copy in copies:
        copy.start()
    tiles = depth // lanes

    def face(out, outer, inner, factor, count, tiled=False):
        line[:, 0:pad, :] = jnp.zeros((tiles, pad, lanes), f32)
        line[:, pad + count : 2 * pad + count, :] = jnp.zeros((tiles, pad, lanes), f32)
        own = [outer(k) for k in range(tiles)]
        for k in range(tiles):
            line[k, pad : pad + count, :] = own[k]
        for k, z_sum in enumerate(along_z(own)):
            beside = line[k, pad - 1 : pad - 1 + count, :] + line[k, pad + 1 : pad + 1 + count, :]
            beside = beside + z_sum + inner(k)
            at = (k, slice(None), slice(None)) if tiled else (slice(None), column(k))
            out[(0,) + at] = own[k]
            out[(1,) + at] = (
                spread_rate * beside + (1.0 - 6.0 * spread_rate) * own[k] + source(own[k], factor(k))
            )

    for n in range(4):
        copies[n].wait()
    face(x_lo, lambda k: s_rows[0, 0, :, column(k)], lambda k: s_rows[0, 1, :, column(k)],
         lambda k: p_rows[0, 0, :, column(k)], cells_y)
    face(x_hi, lambda k: s_rows[1, 1, :, column(k)], lambda k: s_rows[1, 0, :, column(k)],
         lambda k: p_rows[1, 0, :, column(k)], cells_y)
    for n in range(4, 8):
        copies[n].wait()
    face(y_lo, lambda k: s_cols[0, :, 0, column(k)], lambda k: s_cols[0, :, 1, column(k)],
         lambda k: p_cols[0, :, 0, column(k)], cells_x, True)
    face(y_hi, lambda k: s_cols[1, :, 7, column(k)], lambda k: s_cols[1, :, 6, column(k)],
         lambda k: p_cols[1, :, 7, column(k)], cells_x, True)


def faces(scalar, prefactor):
    cells_x, cells_y, depth = scalar.shape
    x_face = jax.ShapeDtypeStruct((2, cells_y, depth), f32)
    y_face = jax.ShapeDtypeStruct((2, depth // lanes, cells_x, lanes), f32)
    longest = max(cells_x, cells_y)
    return pl.pallas_call(
        faces_kernel,
        out_shape=(x_face, x_face, y_face, y_face),
        in_specs=[anywhere, anywhere],
        out_specs=[in_vmem] * 4,
        scratch_shapes=[
            pltpu.VMEM((2, 2, cells_y, depth), f32),
            pltpu.VMEM((2, 1, cells_y, depth), f32),
            pltpu.VMEM((2, cells_x, 8, depth), f32),
            pltpu.VMEM((2, cells_x, 8, depth), f32),
            pltpu.VMEM((depth // lanes, longest + 2 * pad, lanes), f32),
            pltpu.SemaphoreType.DMA((8,)),
        ],
        name="faces",
    )(scalar, prefactor)


def rows_kernel(
    first_row, rows, flags, scalar, prefactor, x_lo, x_hi, y_lo, y_hi, c_lo, c_hi, factor_z, mix, *rest
):
    (advanced, keep, send, s_buf, p_buf, m_buf, a_buf, low_buf, z_buf, e_buf, s_sem, p_sem, a_sem, e_sem) = rest[-14:]
    cells_x, cells_y, depth = scalar.shape
    tiles = depth // lanes
    inner = pl.ds(pad, cells_y)
    at_lo, at_hi = first_row == 0, first_row + rows == cells_x
    first_slot, end_slot = (2 if at_lo else 0), (rows + 2 if at_hi else rows + 4)
    first_m, end_m = (1 if at_lo else 0), (rows + 1 if at_hi else rows + 2)

    def s_copy(slot, k):
        return pltpu.make_async_copy(
            scalar.at[first_row - 2 + slot, :, pl.ds(k * lanes, lanes)], s_buf.at[k, slot, inner], s_sem.at[slot, k]
        )

    def p_copy(slot):
        return pltpu.make_async_copy(prefactor.at[first_row - 1 + slot], p_buf.at[slot], p_sem.at[slot])

    def a_copy(row):
        return pltpu.make_async_copy(a_buf.at[row], advanced.at[first_row + row], a_sem.at[row])

    def edge_copies(face, slot, n):
        return [
            pltpu.make_async_copy(
                face.at[0, :, pl.ds(k * lanes, lanes)], s_buf.at[k, slot, inner], s_sem.at[slot, k]
            )
            for k in range(tiles)
        ] + [pltpu.make_async_copy(face.at[1], e_buf.at[n], e_sem.at[n])]

    def start(slot, carry):
        for k in range(tiles):
            s_copy(slot, k).start()

        @pl.when(jnp.logical_and(slot - 1 >= first_m, slot - 1 < end_m))
        def _():
            p_copy(slot - 1).start()

        return carry

    if at_lo:
        for copy in edge_copies(x_lo, 1, 0):
            copy.start()
    lax.fori_loop(first_slot, end_slot, start, 0)
    if at_hi:
        for copy in edge_copies(x_hi, rows + 2, 1):
            copy.start()

    def y_rows(slot):
        row = first_row - 2 + slot
        for k in range(tiles):
            s_buf[k, slot, pad - 1 : pad, :] = y_lo[0, k, pl.ds(row, 1), :]
            s_buf[k, slot, pad + cells_y : pad + cells_y + 1, :] = y_hi[0, k, pl.ds(row, 1), :]

    def neighbours(buf, slot):
        own = [buf[k, slot, inner, :] for k in range(tiles)]
        sums = []
        for k, z_sum in enumerate(along_z(own)):
            beside = buf[k, slot - 1, inner, :] + buf[k, slot + 1, inner, :]
            beside = beside + (buf[k, slot, pl.ds(pad - 1, cells_y), :] + buf[k, slot, pl.ds(pad + 1, cells_y), :])
            sums.append(beside + z_sum)
        return own, sums

    def stage_one(slot):
        y_rows(slot + 1)
        own, sums = neighbours(s_buf, slot + 1)
        for k in range(tiles):
            middle = spread_rate * sums[k] + (
                (1.0 - 6.0 * spread_rate) * own[k] + source(own[k], p_buf[slot, :, column(k)])
            )
            m_buf[k, slot, inner, :] = middle

    def m_rows(slot):
        row = first_row - 1 + slot
        for k in range(tiles):
            m_buf[k, slot, pad - 1 : pad, :] = (
                y_lo[1, k, pl.ds(row, 1), :] + flags[2] * s_buf[k, slot + 1, pad : pad + 1, :]
            )
            m_buf[k, slot, pad + cells_y : pad + cells_y + 1, :] = (
                y_hi[1, k, pl.ds(row, 1), :]
                + flags[3] * s_buf[k, slot + 1, pad + cells_y - 1 : pad + cells_y, :]
            )

    def stage_two(row):
        slot = row + 1
        own, sums = neighbours(m_buf, slot)
        for k in range(tiles):
            value = source(own[k], p_buf[slot, :, column(k)]) + s_buf[k, slot + 1, inner, :]
            value = 0.5 * (value + (spread_rate * sums[k] + (1.0 - 6.0 * spread_rate) * own[k]))
            a_buf[row, :, column(k)] = value
            low_buf[row, :, column(k)] = value.astype(bf16)

    def wait_s(slot):
        for k in range(tiles):
            s_copy(slot, k).wait()

    def corner(buf_row, slot, index):
        for k in range(tiles):
            m_buf[k, slot, pad : pad + 1, :] += spread_rate * c_lo[index : index + 1, column(k)]
            end = pad + cells_y
            m_buf[k, slot, end - 1 : end, :] += spread_rate * c_hi[index : index + 1, column(k)]

    def edge(n, slot, beside, index):
        for k in range(tiles):
            m_buf[k, slot, inner, :] = e_buf[n, :, column(k)] + flags[n] * s_buf[k, beside, inner, :]
        corner(None, slot, index)

    def ends(slot, index):
        for k in range(tiles):
            m_buf[k, slot, pad - 1 : pad, :] += spread_rate * c_lo[index : index + 1, column(k)]
            end = pad + cells_y
            m_buf[k, slot, end : end + 1, :] += spread_rate * c_hi[index : index + 1, column(k)]

    if at_lo:
        for copy in edge_copies(x_lo, 1, 0):
            copy.wait()
        wait_s(2)
        wait_s(3)
        p_copy(1).wait()
        edge(0, 0, 2, 0)
        stage_one(1)
        m_rows(1)
        ends(1, 0)
    else:
        for slot in range(4):
            wait_s(slot)
        for slot in range(2):
            p_copy(slot).wait()
            stage_one(slot)
        m_rows(1)

    def step(t, carry):
        wait_s(t + 2)
        p_copy(t).wait()
        stage_one(t)
        m_rows(t)
        stage_two(t - 2)
        a_copy(t - 2).start()
        return carry

    if at_hi:
        lax.fori_loop(2, rows, step, 0)
        for copy in edge_copies(x_hi, rows + 2, 1):
            copy.wait()
        p_copy(rows).wait()
        stage_one(rows)
        m_rows(rows)
        ends(rows, 1)
        stage_two(rows - 2)
        a_copy(rows - 2).start()
        edge(1, rows + 1, rows + 1, 1)
    else:
        lax.fori_loop(2, rows + 1, step, 0)
        wait_s(rows + 3)
        p_copy(rows + 1).wait()
        stage_one(rows + 1)
    stage_two(rows - 1)
    a_copy(rows - 1).start()

    half = keep.shape[1]
    for row in range(rows):
        z_buf[row] = jnp.dot(low_buf[row], factor_z[...], preferred_element_type=f32)
    for row in range(rows):
        z = z_buf[row]
        high = z.astype(bf16)
        low = (z - high.astype(f32)).astype(bf16)
        y = jnp.dot(mix[...], jnp.concatenate([high, low, high], axis=0), preferred_element_type=f32)
        keep[row] = y[:half]
        send[row] = y[half:]

    def finish(row, carry):
        a_copy(row).wait()
        return carry

    lax.fori_loop(0, rows, finish, 0)


def run_of_rows(index, rows, flags, scalar, prefactor, halos, factor_z, mix, previous):
    cells_x, cells_y, depth = scalar.shape
    ranks = mix.shape[0]
    z_rank = factor_z.shape[1]
    tiles = depth // lanes
    part = jax.ShapeDtypeStruct((rows, ranks // 2, z_rank), f32)
    x_lo, x_hi, y_lo, y_hi, c_lo, c_hi = halos
    operands = [flags, scalar, prefactor, x_lo, x_hi, y_lo, y_hi, c_lo, c_hi, factor_z, mix]
    specs = [pl.BlockSpec(memory_space=pltpu.SMEM)] + [anywhere] * 4 + [in_vmem] * 6
    aliases = {}
    if previous is not None:
        operands.append(previous)
        specs.append(anywhere)
        aliases = {len(operands) - 1: 0}
    plane = (cells_y + 2 * pad, lanes)
    cells = rows * cells_y * depth
    return pl.pallas_call(
        functools.partial(rows_kernel, index * rows, rows),
        out_shape=(jax.ShapeDtypeStruct(scalar.shape, f32), part, part),
        in_specs=specs,
        out_specs=[anywhere, in_vmem, in_vmem],
        input_output_aliases=aliases,
        scratch_shapes=[
            pltpu.VMEM((tiles, rows + 4) + plane, f32),
            pltpu.VMEM((rows + 2, cells_y, depth), f32),
            pltpu.VMEM((tiles, rows + 2) + plane, f32),
            pltpu.VMEM((rows, cells_y, depth), f32),
            pltpu.VMEM((rows, cells_y, depth), bf16),
            pltpu.VMEM((rows, cells_y, z_rank), f32),
            pltpu.VMEM((2, cells_y, depth), f32),
            pltpu.SemaphoreType.DMA((rows + 4, tiles)),
            pltpu.SemaphoreType.DMA((rows + 2,)),
            pltpu.SemaphoreType.DMA((rows,)),
            pltpu.SemaphoreType.DMA((2,)),
        ],
        cost_estimate=pl.CostEstimate(
            flops=60 * cells + 2 * cells * z_rank, bytes_accessed=12 * cells, transcendentals=4 * cells
        ),
        name=f"rows_{index}",
    )(*operands)


def shift(array, axis, step):
    peers = lax.axis_size(axis)
    return lax.ppermute(array, axis, [(i, i + step) for i in range(peers) if 0 <= i + step < peers])


def swap(array, axis, distance):
    return lax.ppermute(array, axis, [(i, i ^ distance) for i in range(lax.axis_size(axis))])


def gathered(array, axis):
    peers, distance = lax.axis_size(axis), 1
    me = lax.axis_index(axis)
    while distance < peers:
        other = swap(array, axis, distance)
        upper = (me & distance) != 0
        array = jnp.concatenate([jnp.where(upper, other, array), jnp.where(upper, array, other)], axis=0)
        distance *= 2
    return array


def split(array):
    high = lax.reduce_precision(array, 8, 7)
    return high.astype(bf16), (array - high).astype(bf16)


def on_device(scalar, prefactor, factor_x, factor_y, factor_z):
    cells_x, cells_y, depth = scalar.shape
    peers_x, peers_y = lax.axis_size("gx"), lax.axis_size("gy")
    at_x, at_y = lax.axis_index("gx"), lax.axis_index("gy")
    y_rank, z_rank = factor_y.shape[1], factor_z.shape[1]
    block = y_rank // peers_y

    x_lo, x_hi, y_lo, y_hi = faces(scalar, prefactor)
    from_x_lo, from_x_hi = shift(x_hi, "gx", 1), shift(x_lo, "gx", -1)
    from_y_lo, from_y_hi = shift(y_hi, "gy", 1), shift(y_lo, "gy", -1)
    beside = jnp.stack([from_x_lo[0], from_x_hi[0]])
    c_lo = shift(beside[:, cells_y - 1], "gy", 1)
    c_hi = shift(beside[:, 0], "gy", -1)
    halos = (from_x_lo, from_x_hi, from_y_lo, from_y_hi, c_lo, c_hi)
    flags = spread_rate * jnp.stack(
        [at_x > 0, at_x < peers_x - 1, at_y > 0, at_y < peers_y - 1]
    ).astype(f32)

    bits = peers_y.bit_length() - 1
    order = jnp.array([int(format(n, f"0{bits}b")[::-1], 2) if bits else 0 for n in range(peers_y)])
    blocks = factor_y.T.reshape(peers_y, block, cells_y)
    ordered = jnp.take(blocks, order ^ at_y, axis=0).reshape(y_rank, cells_y)
    high, low = split(ordered)
    mix = jnp.concatenate([high, high, low], axis=1)

    all_x = gathered(factor_x, "gx")

    rows = cells_x // chunks
    advanced, owned = None, []
    for index in range(chunks):
        advanced, keep, send = run_of_rows(
            index, rows, flags, scalar, prefactor, halos, factor_z, mix, advanced
        )
        distance = 1
        while True:
            keep = keep + swap(send, "gy", distance)
            distance *= 2
            if distance == peers_y:
                break
            half = keep.shape[1] // 2
            keep, send = keep[:, :half], keep[:, half:]
        owned.append(keep)
    owned = jnp.concatenate(owned, axis=0)

    columns = block * z_rank // peers_x
    parts = owned.reshape(cells_x, peers_x, columns).transpose(1, 0, 2)
    parts = lax.all_to_all(parts, "gx", 0, 0, tiled=True).reshape(peers_x * cells_x, columns)
    core = jnp.einsum("xa,xn->an", all_x, parts, precision=lax.Precision.HIGHEST)
    core = core.reshape(peers_x, -1, columns)
    core = lax.all_to_all(core, "gx", 0, 0, tiled=True)
    core = core.transpose(1, 0, 2).reshape(-1, block, z_rank)
    return (advanced, core)


def solution(mesh):
    return jax.shard_map(
        on_device,
        mesh=mesh,
        in_specs=(P("gx", "gy", None), P("gx", "gy", None), P("gx", None), P("gy", None), P()),
        out_specs=(P("gx", "gy", None), P("gx", "gy", None)),
        check_vma=False,
    )
```

```python
import functools
import math

import jax
import jax.numpy as jnp
from jax import lax
from jax.experimental import pallas as pl
from jax.experimental.pallas import tpu as pltpu
from jax.sharding import PartitionSpec as P

spread_rate = 0.12
kept_rate = 1.0 - 6.0 * spread_rate
activation = 2.0
exponent = -activation * math.log2(math.e)
lanes = 128
pad = 8
group = 4
f32, bf16 = jnp.float32, jnp.bfloat16
room = pltpu.CompilerParams(vmem_limit_bytes=58 << 20)
in_hbm = pl.BlockSpec(memory_space=pltpu.HBM)
in_vmem = pl.BlockSpec(memory_space=pltpu.VMEM)


def source(field, prefactor):
    return prefactor * jnp.exp2(exponent / (1.0 + field * field))


def along_z(tiles):
    lane = lax.broadcasted_iota(jnp.int32, tiles[0].shape, 1)
    last = len(tiles) - 1
    sums = []
    for k, tile in enumerate(tiles):
        below = tiles[k - 1] if k else 0.0
        above = tiles[k + 1] if k < last else 0.0
        left = pltpu.roll(jnp.where(lane == lanes - 1, below, tile), 1, 1)
        right = pltpu.roll(jnp.where(lane == 0, above, tile), lanes - 1, 1)
        sums.append(left + right)
    return sums


def column(k):
    return slice(k * lanes, (k + 1) * lanes)


def neighbours(buf, slot, count):
    own = [buf[k, slot, pl.ds(pad, count), :] for k in range(buf.shape[0])]
    sums = []
    for k, z_sum in enumerate(along_z(own)):
        beside = buf[k, slot - 1, pl.ds(pad, count), :] + buf[k, slot + 1, pl.ds(pad, count), :]
        beside = beside + (buf[k, slot, pl.ds(pad - 1, count), :] + buf[k, slot, pl.ds(pad + 1, count), :])
        sums.append(beside + z_sum)
    return own, sums


def faces_kernel(peers_y, scalar, prefactor, factor_y, y_lo, y_hi, mix, s_cols, p_cols, line, turned, sems):
    cells_x, cells_y, depth = scalar.shape
    tiles = depth // lanes

    def copies_of(n, source, first_y, buf, side):
        return [
            pltpu.make_async_copy(
                source.at[:, pl.ds(first_y, 8), pl.ds(k * lanes, lanes)],
                buf.at[side, k].reshape(cells_x, 8, lanes),
                sems.at[n, k],
            )
            for k in range(tiles)
        ]

    copies = [
        copies_of(0, scalar, 0, s_cols, 0),
        copies_of(1, prefactor, 0, p_cols, 0),
        copies_of(2, scalar, cells_y - 8, s_cols, 1),
        copies_of(3, prefactor, cells_y - 8, p_cols, 1),
    ]
    for some in copies:
        for one in some:
            one.start()

    ranks = factor_y.shape[1]
    block = ranks // peers_y
    turned[...] = factor_y[...].T
    at_y = lax.axis_index("gy")
    bits = peers_y.bit_length() - 1
    for n in range(peers_y):
        other = int(format(n, f"0{bits}b")[::-1], 2) if bits else 0
        rows = turned[pl.ds(pl.multiple_of((at_y ^ other) * block, block), block), :]
        high = rows.astype(bf16)
        low = (rows - high.astype(f32)).astype(bf16)
        mix[n * block : (n + 1) * block, :] = jnp.concatenate([high, high, low], axis=1)

    for k in range(tiles):
        line[k, 0:pad, :] = jnp.zeros((pad, lanes), f32)
        line[k, pad + cells_x :, :] = jnp.zeros((pad, lanes), f32)
    for side, (out, edge, next_in) in enumerate(((y_lo, 0, 1), (y_hi, 7, 6))):
        for one in copies[2 * side] + copies[2 * side + 1]:
            one.wait()

        def cells(buf, y, k):
            return buf[side, k, pl.ds(y, cells_x, stride=8), :]

        own = [cells(s_cols, edge, k) for k in range(tiles)]
        for k in range(tiles):
            line[k, pad : pad + cells_x, :] = own[k]
        for k, z_sum in enumerate(along_z(own)):
            beside = line[k, pad - 1 : pad - 1 + cells_x, :] + line[k, pad + 1 : pad + 1 + cells_x, :]
            beside = beside + z_sum + cells(s_cols, next_in, k)
            out[0, k] = spread_rate * own[k]
            out[1, k] = spread_rate * beside + (kept_rate * own[k] + source(own[k], cells(p_cols, edge, k)))


def faces(scalar, prefactor, factor_y):
    cells_x, cells_y, depth = scalar.shape
    ranks = factor_y.shape[1]
    face = jax.ShapeDtypeStruct((2, depth // lanes, cells_x, lanes), f32)
    factors = jax.ShapeDtypeStruct((ranks, 3 * cells_y), bf16)
    return pl.pallas_call(
        functools.partial(faces_kernel, lax.axis_size("gy")),
        out_shape=(face, face, factors),
        in_specs=[in_hbm, in_hbm, in_vmem],
        out_specs=[in_vmem] * 3,
        scratch_shapes=[
            pltpu.VMEM((2, depth // lanes, cells_x * 8, lanes), f32),
            pltpu.VMEM((2, depth // lanes, cells_x * 8, lanes), f32),
            pltpu.VMEM((depth // lanes, cells_x + 2 * pad, lanes), f32),
            pltpu.VMEM((ranks, cells_y), f32),
            pltpu.SemaphoreType.DMA((4, depth // lanes)),
        ],
        compiler_params=room,
        name="faces",
    )(scalar, prefactor, factor_y)


def first_kernel(scalar, prefactor, after, middle, s_buf, p_buf, m_buf, s_sem, p_sem, m_sem):
    cells_x, cells_y, depth = scalar.shape
    tiles = depth // lanes
    groups = cells_x // group

    def s_copy(g, k):
        return pltpu.make_async_copy(
            scalar.at[pl.ds(g * group, group), :, pl.ds(k * lanes, lanes)],
            s_buf.at[k, pl.ds(g * group + 1, group), pl.ds(pad, cells_y)],
            s_sem.at[g, k],
        )

    def p_copy(g):
        rows = pl.ds(g * group, group)
        return pltpu.make_async_copy(prefactor.at[rows], p_buf.at[rows], p_sem.at[g])

    def m_copy(g):
        rows = pl.ds(g * group, group)
        return pltpu.make_async_copy(m_buf.at[:, rows], middle.at[:, rows], m_sem.at[g])

    def start(g, carry):
        for k in range(tiles):
            s_copy(g, k).start()
        p_copy(g).start()
        return carry

    lax.fori_loop(0, groups, start, 0)

    for k in range(tiles):
        s_buf[k, 0, pad : pad + cells_y, :] = jnp.zeros((cells_y, lanes), f32)
        s_buf[k, cells_x + 1, pad : pad + cells_y, :] = jnp.zeros((cells_y, lanes), f32)

    def wait_s(g):
        for k in range(tiles):
            s_copy(g, k).wait()

    def row_of(row):
        for k in range(tiles):
            s_buf[k, row + 1, 0:pad, :] = jnp.zeros((pad, lanes), f32)
            s_buf[k, row + 1, pad + cells_y :, :] = jnp.zeros((pad, lanes), f32)
        own, sums = neighbours(s_buf, row + 1, cells_y)
        for k in range(tiles):
            m_buf[k, row] = spread_rate * sums[k] + (kept_rate * own[k] + source(own[k], p_buf[row, :, column(k)]))

    def rows_of(g):
        p_copy(g).wait()

        def one(r, carry):
            row_of(g * group + r)
            return carry

        lax.fori_loop(0, group, one, 0, unroll=True)
        m_copy(g).start()

    wait_s(0)

    def step(g, carry):
        wait_s(g + 1)
        rows_of(g)
        return carry

    lax.fori_loop(0, groups - 1, step, 0)
    rows_of(groups - 1)

    def finish(g, carry):
        m_copy(g).wait()
        return carry

    lax.fori_loop(0, groups, finish, 0)


def first_stage(scalar, prefactor, after):
    cells_x, cells_y, depth = scalar.shape
    tiles, cells = depth // lanes, math.prod(scalar.shape)
    groups = cells_x // group
    return pl.pallas_call(
        first_kernel,
        out_shape=jax.ShapeDtypeStruct((tiles, cells_x, cells_y, lanes), f32),
        in_specs=[in_hbm] * 3,
        out_specs=in_hbm,
        scratch_shapes=[
            pltpu.VMEM((tiles, cells_x + 2, cells_y + 2 * pad, lanes), f32),
            pltpu.VMEM((cells_x, cells_y, depth), f32),
            pltpu.VMEM((tiles, cells_x, cells_y, lanes), f32),
            pltpu.SemaphoreType.DMA((groups, tiles)),
            pltpu.SemaphoreType.DMA((groups,)),
            pltpu.SemaphoreType.DMA((groups,)),
        ],
        cost_estimate=pl.CostEstimate(flops=24 * cells, bytes_accessed=12 * cells, transcendentals=2 * cells),
        compiler_params=room,
        name="first_stage",
    )(scalar, prefactor, after)


def second_kernel(first_row, rows, n_extra, sends, peers, middle, scalar, prefactor, y_lo_in, y_hi_in, factor_z_in, mix_in, *rest):
    (m_buf, s_buf, p_buf, a_buf, low_buf, z_buf, y_lo, y_hi, factor_z, mix, face, m_sem, s_sem, p_sem, a_sem, x_sem, y_sem) = rest[-17:]
    messages = rest[-19:-17] if sends else ()
    (advanced, keep, send) = rest[-22:-19] if sends else rest[-20:-17]
    cells_x, cells_y, depth = scalar.shape
    tiles = depth // lanes
    at_lo, at_hi = first_row == 0, first_row + rows == cells_x
    end = pad + cells_y
    half = keep.shape[1]
    at_x, at_y = lax.axis_index("gx"), lax.axis_index("gy")

    def share(there):
        return jnp.where(there, spread_rate, 0.0).astype(f32)

    y_shares = (share(at_y > 0), share(at_y < peers[1] - 1))

    def m_copy(slot):
        return pltpu.make_async_copy(
            middle.at[:, first_row - 1 + slot], m_buf.at[:, slot, pl.ds(pad, cells_y)], m_sem.at[slot]
        )

    def s_copy(row):
        return pltpu.make_async_copy(scalar.at[first_row + row], s_buf.at[row], s_sem.at[row])

    def p_copy(row):
        return pltpu.make_async_copy(prefactor.at[first_row + row], p_buf.at[row], p_sem.at[row])

    def a_copy(row):
        return pltpu.make_async_copy(a_buf.at[row], advanced.at[first_row + row], a_sem.at[row])

    def start(row, carry):
        m_copy(row + 1).start()
        s_copy(row).start()
        p_copy(row).start()
        return carry

    small = [(y_lo_in, y_lo), (y_hi_in, y_hi), (factor_z_in, factor_z), (mix_in, mix)]
    small += [(rest[0], face)] * n_extra
    small = [pltpu.make_async_copy(a, b, y_sem.at[n]) for n, (a, b) in enumerate(small)]
    if not at_lo:
        m_copy(0).start()
    for row in range(2):
        start(row, 0)
    for copy in small:
        copy.start()
    lax.fori_loop(2, rows, start, 0)
    if not at_hi:
        m_copy(rows + 1).start()

    for copy in small:
        copy.wait()

    x_copies = []
    for n, message in enumerate(messages):
        row = n * (cells_x - 1)
        for k in range(tiles):
            x_copies.append(
                pltpu.make_async_copy(
                    scalar.at[row, :, pl.ds(k * lanes, lanes)], message.at[k, pl.ds(0, cells_y)], x_sem.at[n, k]
                )
            )
            message[k, 2 * cells_y : 2 * cells_y + 1, :] = y_lo[0, k, row : row + 1, :]
            message[k, 2 * cells_y + 1 : 2 * cells_y + 2, :] = y_hi[0, k, row : row + 1, :]
        x_copies.append(
            pltpu.make_async_copy(
                middle.at[:, row], message.at[:, pl.ds(cells_y, cells_y)], x_sem.at[n, tiles]
            )
        )
    for copy in x_copies:
        copy.start()

    def add(k, slot, y, value):
        m_buf[k, slot, pl.ds(y, 1), :] = m_buf[k, slot, pl.ds(y, 1), :] + value

    def settle(slot):
        row = first_row - 1 + slot
        for k in range(tiles):
            add(k, slot, pad, y_lo[0, k, pl.ds(row, 1), :])
            add(k, slot, end - 1, y_hi[0, k, pl.ds(row, 1), :])

    def beside_y(slot):
        row = first_row - 1 + slot
        for k in range(tiles):
            m_buf[k, slot, pad - 1 : pad, :] = (
                y_lo[1, k, pl.ds(row, 1), :] + y_shares[0] * s_buf[slot - 1, 0:1, column(k)]
            )
            m_buf[k, slot, end : end + 1, :] = (
                y_hi[1, k, pl.ds(row, 1), :] + y_shares[1] * s_buf[slot - 1, cells_y - 1 : cells_y, column(k)]
            )

    def edge(there, slot, own_slot):
        part = share(there)
        for k in range(tiles):
            m_buf[k, slot, pad:end, :] = face[k, cells_y : 2 * cells_y, :] + part * s_buf[own_slot - 1, :, column(k)]
            m_buf[k, own_slot, pad:end, :] = m_buf[k, own_slot, pad:end, :] + spread_rate * face[k, :cells_y, :]
            below, above = face[k, 2 * cells_y : 2 * cells_y + 1, :], face[k, 2 * cells_y + 1 : 2 * cells_y + 2, :]
            add(k, slot, pad, below)
            add(k, slot, end - 1, above)
            add(k, own_slot, pad - 1, below)
            add(k, own_slot, end, above)

    def dot_z(row):
        z_buf[row] = jnp.dot(low_buf[row], factor_z[...], preferred_element_type=f32)

    def dot_y(row):
        z = z_buf[row]
        high = z.astype(bf16)
        low = (z - high.astype(f32)).astype(bf16)
        y = jnp.dot(mix[...], jnp.concatenate([high, low, high], axis=0), preferred_element_type=f32)
        keep[row] = y[:half]
        send[row] = y[half:]

    def advance(row):
        slot = row + 1
        own, sums = neighbours(m_buf, slot, cells_y)
        for k in range(tiles):
            value = source(own[k], p_buf[row, :, column(k)]) + s_buf[row, :, column(k)]
            value = 0.5 * (value + (spread_rate * sums[k] + kept_rate * own[k]))
            a_buf[row, :, column(k)] = value
            low_buf[row, :, column(k)] = value.astype(bf16)

    if not at_lo:
        m_copy(0).wait()
        settle(0)
    for row in range(2):
        s_copy(row).wait()
        m_copy(row + 1).wait()
        settle(row + 1)
        beside_y(row + 1)
    if at_lo:
        edge(at_x > 0, 0, 1)

    def step(n, carry):
        t = 2 * n
        for row in (t, t + 1):
            p_copy(row).wait()
            s_copy(row + 2).wait()
            m_copy(row + 3).wait()
        for row in (t, t + 1):
            dot_y(jnp.maximum(row - 4, 0))
        for row in (t, t + 1):
            dot_z(jnp.maximum(row - 2, 0))
        for row in (t, t + 1):
            settle(row + 3)
            beside_y(row + 3)
        for row in (t, t + 1):
            advance(row)
        for row in (t, t + 1):
            a_copy(row).start()
        return carry

    lax.fori_loop(0, rows // 2 - 1, step, 0)
    if at_hi:
        edge(at_x < peers[0] - 1, rows + 1, rows)
    else:
        m_copy(rows + 1).wait()
        settle(rows + 1)
    last = range(rows - 2, rows)
    for row in last:
        p_copy(row).wait()
    for row in last:
        dot_y(row - 4)
    for row in last:
        dot_z(row - 2)
    for row in last:
        advance(row)
    for row in last:
        a_copy(row).start()
    for row in last:
        dot_y(row - 2)
    for row in last:
        dot_z(row)
    for row in last:
        dot_y(row)

    def finish(row, carry):
        a_copy(row).wait()
        return carry

    lax.fori_loop(0, rows, finish, 0)
    for copy in x_copies:
        copy.wait()


def second_stage(first_row, rows, middle, scalar, prefactor, y_lo, y_hi, factor_z, mix, beside, previous, after, sends):
    _, cells_y, depth = scalar.shape
    ranks, z_rank = mix.shape[0], factor_z.shape[1]
    tiles, cells = depth // lanes, rows * cells_y * depth
    part = jax.ShapeDtypeStruct((rows, ranks // 2, z_rank), f32)
    messages = [jax.ShapeDtypeStruct((tiles, 2 * cells_y + pad, lanes), f32)] * (2 * sends)
    operands = [middle, scalar, prefactor, y_lo, y_hi, factor_z, mix, *beside]
    specs = [in_hbm] * (7 + len(beside))
    aliases = {}
    if previous is not None:
        aliases = {len(operands): 0}
        operands.append(previous)
        specs.append(in_hbm)
    operands += after
    specs += [in_hbm] * len(after)
    return pl.pallas_call(
        functools.partial(
            second_kernel, first_row, rows, len(beside), sends, (lax.axis_size("gx"), lax.axis_size("gy"))
        ),
        out_shape=(jax.ShapeDtypeStruct(scalar.shape, f32), part, part, *messages),
        in_specs=specs,
        out_specs=[in_hbm] + [in_vmem] * (2 + len(messages)),
        input_output_aliases=aliases,
        scratch_shapes=[
            pltpu.VMEM((tiles, rows + 2, cells_y + 2 * pad, lanes), f32),
            pltpu.VMEM((rows + 1, cells_y, depth), f32),
            pltpu.VMEM((rows, cells_y, depth), f32),
            pltpu.VMEM((rows, cells_y, depth), f32),
            pltpu.VMEM((rows, cells_y, depth), bf16),
            pltpu.VMEM((rows, cells_y, z_rank), f32),
            pltpu.VMEM(y_lo.shape, f32),
            pltpu.VMEM(y_hi.shape, f32),
            pltpu.VMEM(factor_z.shape, factor_z.dtype),
            pltpu.VMEM(mix.shape, bf16),
            pltpu.VMEM((tiles, 2 * cells_y + pad, lanes), f32),
            pltpu.SemaphoreType.DMA((rows + 2,)),
            pltpu.SemaphoreType.DMA((rows,)),
            pltpu.SemaphoreType.DMA((rows,)),
            pltpu.SemaphoreType.DMA((rows,)),
            pltpu.SemaphoreType.DMA((2, tiles + 1)),
            pltpu.SemaphoreType.DMA((5,)),
        ],
        cost_estimate=pl.CostEstimate(
            flops=30 * cells + 2 * cells * z_rank, bytes_accessed=16 * cells, transcendentals=2 * cells
        ),
        compiler_params=room,
    )(*operands)


def shift(array, axis, step):
    peers = lax.axis_size(axis)
    return lax.ppermute(array, axis, [(i, i + step) for i in range(peers) if 0 <= i + step < peers])


def swap(array, axis, distance):
    return lax.ppermute(array, axis, [(i, i ^ distance) for i in range(lax.axis_size(axis))])


def gathered(array, axis):
    peers = lax.axis_size(axis)
    me, distance, place = lax.axis_index(axis), peers // 2, 0
    while distance:
        other = swap(array, axis, distance)
        upper = (me & distance) != 0
        array = jnp.stack([jnp.where(upper, other, array), jnp.where(upper, array, other)], axis=place)
        distance, place = distance // 2, place + 1
    return array.reshape((-1,) + array.shape[-1:])


def runs_of(cells_x):
    eighth = cells_x // 8
    return [(eighth, 4 * eighth), (5 * eighth, 3 * eighth), (0, eighth)]


def on_device(scalar, prefactor, factor_x, factor_y, factor_z):
    cells_x, _, _ = scalar.shape
    peers_x, peers_y = lax.axis_size("gx"), lax.axis_size("gy")
    y_rank, z_rank = factor_y.shape[1], factor_z.shape[1]
    block = y_rank // peers_y

    to_y_lo, to_y_hi, mix = faces(scalar, prefactor, factor_y)
    y_lo, y_hi = shift(to_y_hi, "gy", 1), shift(to_y_lo, "gy", -1)
    middle = first_stage(scalar, prefactor, to_y_lo)

    def halved(run):
        number, held, coming, distance = run
        held = held + coming
        if 2 * distance == peers_y:
            owned[number] = held
            return []
        half = held.shape[1] // 2
        coming = swap(held[:, half:], "gy", 2 * distance)
        return [(number, held[:, :half], coming, 2 * distance)]

    all_x = gathered(factor_x, "gx")
    runs = runs_of(cells_x)
    advanced, owned, in_flight = None, {}, []
    for number, (first_row, rows) in enumerate(runs):
        beside = [x_lo] * (first_row == 0) + [x_hi] * (first_row + rows == cells_x) if number else []
        advanced, keep, send, *messages = second_stage(
            first_row, rows, middle, scalar, prefactor, y_lo, y_hi, factor_z, mix, beside, advanced, [], not number
        )
        in_flight = sum((halved(run) for run in in_flight), [])
        in_flight.append((number, keep, swap(send, "gy", 1), 1))
        if messages:
            x_lo = shift(messages[1], "gx", 1)
            x_hi = shift(messages[0], "gx", -1)
    while in_flight:
        in_flight = sum((halved(run) for run in in_flight), [])
    owned = jnp.concatenate([owned[number] for number in sorted(owned, key=lambda n: runs[n][0])], axis=0)

    columns = block * z_rank // peers_x
    parts = owned.reshape(cells_x, peers_x, columns).transpose(1, 0, 2)
    parts = lax.all_to_all(parts, "gx", 0, 0, tiled=True).reshape(peers_x * cells_x, columns)
    core = jnp.einsum("xa,xn->an", all_x, parts, precision=lax.Precision.HIGHEST)
    core = core.reshape(peers_x, -1, columns)
    core = lax.all_to_all(core, "gx", 0, 0, tiled=True)
    core = core.transpose(1, 0, 2).reshape(-1, block, z_rank)
    return (advanced, core)


def solution(mesh):
    return jax.shard_map(
        on_device,
        mesh=mesh,
        in_specs=(P("gx", "gy", None), P("gx", "gy", None), P("gx", None), P("gy", None), P()),
        out_specs=(P("gx", "gy", None), P("gx", "gy", None)),
        check_vma=False,
    )
```

```python
import functools
import math

import jax
import jax.numpy as jnp
from jax import lax
from jax.experimental import pallas as pl
from jax.experimental.pallas import tpu as pltpu
from jax.sharding import PartitionSpec as P

spread_rate = 0.12
kept_rate = 1.0 - 6.0 * spread_rate
activation = 2.0
exponent = -activation * math.log2(math.e)
lanes = 128
piece = 32
pad = 8
group = 4
f32, bf16 = jnp.float32, jnp.bfloat16
room = pltpu.CompilerParams(vmem_limit_bytes=58 << 20)
in_hbm = pl.BlockSpec(memory_space=pltpu.HBM)
in_vmem = pl.BlockSpec(memory_space=pltpu.VMEM)


def source(field, prefactor):
    return prefactor * jnp.exp2(exponent / (1.0 + field * field))


def along_z(tiles):
    lane = lax.broadcasted_iota(jnp.int32, tiles[0].shape, 1)
    last = len(tiles) - 1
    sums = []
    for k, tile in enumerate(tiles):
        below = tiles[k - 1] if k else 0.0
        above = tiles[k + 1] if k < last else 0.0
        left = pltpu.roll(jnp.where(lane == lanes - 1, below, tile), 1, 1)
        right = pltpu.roll(jnp.where(lane == 0, above, tile), lanes - 1, 1)
        sums.append(left + right)
    return sums


def column(k):
    return slice(k * lanes, (k + 1) * lanes)


def beside_z(tile, below, above):
    lane = lax.broadcasted_iota(jnp.int32, tile.shape, 1)
    left = pltpu.roll(jnp.where(lane == lanes - 1, below, tile), 1, 1)
    right = pltpu.roll(jnp.where(lane == 0, above, tile), lanes - 1, 1)
    return left + right


def neighbours(buf, slot, k, first, count):
    def cells(k, slot, y):
        return buf[k, slot, pl.ds(pad + y, count), :]

    own = cells(k, slot, first)
    below = cells(k - 1, slot, first) if k else 0.0
    above = cells(k + 1, slot, first) if k < buf.shape[0] - 1 else 0.0
    beside = (cells(k, slot - 1, first) + cells(k, slot + 1, first)) + (
        cells(k, slot, first - 1) + cells(k, slot, first + 1)
    )
    return own, beside + beside_z(own, below, above)


def faces_kernel(peers_y, scalar, prefactor, factor_y, y_lo, y_hi, mix, s_cols, p_cols, line, turned, sems):
    cells_x, cells_y, depth = scalar.shape
    tiles = depth // lanes

    def copies_of(n, source, first_y, buf, side):
        return [
            pltpu.make_async_copy(
                source.at[:, pl.ds(first_y, 8), pl.ds(k * lanes, lanes)],
                buf.at[side, k].reshape(cells_x, 8, lanes),
                sems.at[n, k],
            )
            for k in range(tiles)
        ]

    copies = [
        copies_of(0, scalar, 0, s_cols, 0),
        copies_of(1, prefactor, 0, p_cols, 0),
        copies_of(2, scalar, cells_y - 8, s_cols, 1),
        copies_of(3, prefactor, cells_y - 8, p_cols, 1),
    ]
    for some in copies:
        for one in some:
            one.start()

    ranks = factor_y.shape[1]
    block = ranks // peers_y
    turned[...] = factor_y[...].T
    at_y = lax.axis_index("gy")
    bits = peers_y.bit_length() - 1
    for n in range(peers_y):
        other = int(format(n, f"0{bits}b")[::-1], 2) if bits else 0
        rows = turned[pl.ds(pl.multiple_of((at_y ^ other) * block, block), block), :]
        high = rows.astype(bf16)
        low = (rows - high.astype(f32)).astype(bf16)
        mix[n * block : (n + 1) * block, :] = jnp.concatenate([high, high, low], axis=1)

    for k in range(tiles):
        line[k, 0:pad, :] = jnp.zeros((pad, lanes), f32)
        line[k, pad + cells_x :, :] = jnp.zeros((pad, lanes), f32)
    for side, (out, edge, next_in) in enumerate(((y_lo, 0, 1), (y_hi, 7, 6))):
        for one in copies[2 * side] + copies[2 * side + 1]:
            one.wait()

        def cells(buf, y, k):
            return buf[side, k, pl.ds(y, cells_x, stride=8), :]

        own = [cells(s_cols, edge, k) for k in range(tiles)]
        for k in range(tiles):
            line[k, pad : pad + cells_x, :] = own[k]
        for k, z_sum in enumerate(along_z(own)):
            beside = line[k, pad - 1 : pad - 1 + cells_x, :] + line[k, pad + 1 : pad + 1 + cells_x, :]
            beside = beside + z_sum + cells(s_cols, next_in, k)
            out[0, k] = spread_rate * own[k]
            out[1, k] = spread_rate * beside + (kept_rate * own[k] + source(own[k], cells(p_cols, edge, k)))


def faces(scalar, prefactor, factor_y):
    cells_x, cells_y, depth = scalar.shape
    ranks = factor_y.shape[1]
    face = jax.ShapeDtypeStruct((2, depth // lanes, cells_x, lanes), f32)
    factors = jax.ShapeDtypeStruct((ranks, 3 * cells_y), bf16)
    return pl.pallas_call(
        functools.partial(faces_kernel, lax.axis_size("gy")),
        out_shape=(face, face, factors),
        in_specs=[in_hbm, in_hbm, in_vmem],
        out_specs=[in_vmem] * 3,
        scratch_shapes=[
            pltpu.VMEM((2, depth // lanes, cells_x * 8, lanes), f32),
            pltpu.VMEM((2, depth // lanes, cells_x * 8, lanes), f32),
            pltpu.VMEM((depth // lanes, cells_x + 2 * pad, lanes), f32),
            pltpu.VMEM((ranks, cells_y), f32),
            pltpu.SemaphoreType.DMA((4, depth // lanes)),
        ],
        compiler_params=room,
        name="faces",
    )(scalar, prefactor, factor_y)


def first_kernel(scalar, prefactor, after, middle, s_buf, p_buf, m_buf, s_sem, p_sem, m_sem):
    cells_x, cells_y, depth = scalar.shape
    tiles = depth // lanes
    groups = cells_x // group

    def s_copy(g, k):
        return pltpu.make_async_copy(
            scalar.at[pl.ds(g * group, group), :, pl.ds(k * lanes, lanes)],
            s_buf.at[k, pl.ds(g * group + 1, group), pl.ds(pad, cells_y)],
            s_sem.at[g, k],
        )

    def p_copy(g):
        rows = pl.ds(g * group, group)
        return pltpu.make_async_copy(prefactor.at[rows], p_buf.at[rows], p_sem.at[g])

    def m_copy(g):
        rows = pl.ds(g * group, group)
        return pltpu.make_async_copy(m_buf.at[:, rows], middle.at[:, rows], m_sem.at[g])

    def start(g, carry):
        for k in range(tiles):
            s_copy(g, k).start()
        p_copy(g).start()
        return carry

    lax.fori_loop(0, groups, start, 0)

    for k in range(tiles):
        s_buf[k, 0, pad : pad + cells_y, :] = jnp.zeros((cells_y, lanes), f32)
        s_buf[k, cells_x + 1, pad : pad + cells_y, :] = jnp.zeros((cells_y, lanes), f32)

    def clear(row, carry):
        for k in range(tiles):
            s_buf[k, row + 1, 0:pad, :] = jnp.zeros((pad, lanes), f32)
            s_buf[k, row + 1, pad + cells_y :, :] = jnp.zeros((pad, lanes), f32)
        return carry

    lax.fori_loop(0, cells_x, clear, 0)

    def wait_s(g):
        for k in range(tiles):
            s_copy(g, k).wait()

    pieces = [(k, y) for k in range(tiles) for y in range(0, cells_y, piece)]

    def row_of(row):
        for k, y in pieces:
            own, beside = neighbours(s_buf, row + 1, k, y, piece)
            m_buf[k, row, pl.ds(y, piece), :] = spread_rate * beside + (
                kept_rate * own + source(own, p_buf[row, pl.ds(y, piece), column(k)])
            )

    def rows_of(g):
        p_copy(g).wait()

        def one(r, carry):
            row_of(g * group + r)
            return carry

        lax.fori_loop(0, group, one, 0, unroll=True)
        m_copy(g).start()

    wait_s(0)

    def step(g, carry):
        wait_s(g + 1)
        rows_of(g)
        return carry

    lax.fori_loop(0, groups - 1, step, 0)
    rows_of(groups - 1)

    def finish(g, carry):
        m_copy(g).wait()
        return carry

    lax.fori_loop(0, groups, finish, 0)


def first_stage(scalar, prefactor, after):
    cells_x, cells_y, depth = scalar.shape
    tiles, cells = depth // lanes, math.prod(scalar.shape)
    groups = cells_x // group
    return pl.pallas_call(
        first_kernel,
        out_shape=jax.ShapeDtypeStruct((tiles, cells_x, cells_y, lanes), f32),
        in_specs=[in_hbm] * 3,
        out_specs=in_hbm,
        scratch_shapes=[
            pltpu.VMEM((tiles, cells_x + 2, cells_y + 2 * pad, lanes), f32),
            pltpu.VMEM((cells_x, cells_y, depth), f32),
            pltpu.VMEM((tiles, cells_x, cells_y, lanes), f32),
            pltpu.SemaphoreType.DMA((groups, tiles)),
            pltpu.SemaphoreType.DMA((groups,)),
            pltpu.SemaphoreType.DMA((groups,)),
        ],
        cost_estimate=pl.CostEstimate(flops=24 * cells, bytes_accessed=12 * cells, transcendentals=2 * cells),
        compiler_params=room,
        name="first_stage",
    )(scalar, prefactor, after)


def second_kernel(first_row, rows, n_extra, sends, peers, middle, scalar, prefactor, y_lo_in, y_hi_in, factor_z_in, mix_in, *rest):
    (m_buf, s_buf, p_buf, a_buf, low_buf, z_buf, y_lo, y_hi, factor_z, mix, face, m_sem, s_sem, p_sem, a_sem, x_sem, y_sem) = rest[-17:]
    messages = rest[-19:-17] if sends else ()
    (advanced, keep, send) = rest[-22:-19] if sends else rest[-20:-17]
    cells_x, cells_y, depth = scalar.shape
    tiles = depth // lanes
    at_lo, at_hi = first_row == 0, first_row + rows == cells_x
    end = pad + cells_y
    half = keep.shape[1]
    at_x, at_y = lax.axis_index("gx"), lax.axis_index("gy")

    def share(there):
        return jnp.where(there, spread_rate, 0.0).astype(f32)

    y_shares = (share(at_y > 0), share(at_y < peers[1] - 1))

    def m_copy(slot):
        return pltpu.make_async_copy(
            middle.at[:, first_row - 1 + slot], m_buf.at[:, slot, pl.ds(pad, cells_y)], m_sem.at[slot]
        )

    def s_copy(row):
        return pltpu.make_async_copy(scalar.at[first_row + row], s_buf.at[row], s_sem.at[row])

    def p_copy(row):
        return pltpu.make_async_copy(prefactor.at[first_row + row], p_buf.at[row], p_sem.at[row])

    def a_copy(row):
        return pltpu.make_async_copy(a_buf.at[row], advanced.at[first_row + row], a_sem.at[row])

    def start(row, carry):
        m_copy(row + 1).start()
        s_copy(row).start()
        p_copy(row).start()
        return carry

    small = [(y_lo_in, y_lo), (y_hi_in, y_hi), (factor_z_in, factor_z), (mix_in, mix)]
    small += [(rest[0], face)] * n_extra
    small = [pltpu.make_async_copy(a, b, y_sem.at[n]) for n, (a, b) in enumerate(small)]
    if not at_lo:
        m_copy(0).start()
    for row in range(3):
        start(row, 0)
    for copy in small:
        copy.start()
    lax.fori_loop(3, rows, start, 0)
    if not at_hi:
        m_copy(rows + 1).start()

    for copy in small:
        copy.wait()

    x_copies = []
    for n, message in enumerate(messages):
        row = n * (cells_x - 1)
        for k in range(tiles):
            x_copies.append(
                pltpu.make_async_copy(
                    scalar.at[row, :, pl.ds(k * lanes, lanes)], message.at[k, pl.ds(0, cells_y)], x_sem.at[n, k]
                )
            )
            message[k, 2 * cells_y : 2 * cells_y + 1, :] = y_lo[0, k, row : row + 1, :]
            message[k, 2 * cells_y + 1 : 2 * cells_y + 2, :] = y_hi[0, k, row : row + 1, :]
        x_copies.append(
            pltpu.make_async_copy(
                middle.at[:, row], message.at[:, pl.ds(cells_y, cells_y)], x_sem.at[n, tiles]
            )
        )
    for copy in x_copies:
        copy.start()

    def add(k, slot, y, value):
        m_buf[k, slot, pl.ds(y, 1), :] = m_buf[k, slot, pl.ds(y, 1), :] + value

    def settle(slot):
        row = first_row - 1 + slot
        for k in range(tiles):
            add(k, slot, pad, y_lo[0, k, pl.ds(row, 1), :])
            add(k, slot, end - 1, y_hi[0, k, pl.ds(row, 1), :])

    def beside_y(slot):
        row = first_row - 1 + slot
        for k in range(tiles):
            m_buf[k, slot, pad - 1 : pad, :] = (
                y_lo[1, k, pl.ds(row, 1), :] + y_shares[0] * s_buf[slot - 1, 0:1, column(k)]
            )
            m_buf[k, slot, end : end + 1, :] = (
                y_hi[1, k, pl.ds(row, 1), :] + y_shares[1] * s_buf[slot - 1, cells_y - 1 : cells_y, column(k)]
            )

    def edge(there, slot, own_slot):
        part = share(there)
        for k in range(tiles):
            m_buf[k, slot, pad:end, :] = face[k, cells_y : 2 * cells_y, :] + part * s_buf[own_slot - 1, :, column(k)]
            m_buf[k, own_slot, pad:end, :] = m_buf[k, own_slot, pad:end, :] + spread_rate * face[k, :cells_y, :]
            below, above = face[k, 2 * cells_y : 2 * cells_y + 1, :], face[k, 2 * cells_y + 1 : 2 * cells_y + 2, :]
            add(k, slot, pad, below)
            add(k, slot, end - 1, above)
            add(k, own_slot, pad - 1, below)
            add(k, own_slot, end, above)

    def dot_z(row):
        z_buf[row] = jnp.dot(low_buf[row], factor_z[...], preferred_element_type=f32)

    def dot_y(row):
        z = z_buf[row]
        high = z.astype(bf16)
        low = (z - high.astype(f32)).astype(bf16)
        y = jnp.dot(mix[...], jnp.concatenate([high, low, high], axis=0), preferred_element_type=f32)
        keep[row] = y[:half]
        send[row] = y[half:]

    pieces = [(k, y) for k in range(tiles) for y in range(0, cells_y, piece)]

    def advance(row):
        slot = row + 1
        for k, y in pieces:
            own, beside = neighbours(m_buf, slot, k, y, piece)
            value = source(own, p_buf[row, pl.ds(y, piece), column(k)]) + s_buf[row, pl.ds(y, piece), column(k)]
            value = 0.5 * (value + (spread_rate * beside + kept_rate * own))
            a_buf[row, pl.ds(y, piece), column(k)] = value
            low_buf[row, pl.ds(y, piece), column(k)] = value.astype(bf16)

    for slot in range(4):
        if slot or not at_lo:
            m_copy(slot).wait()
    for row in range(3):
        s_copy(row).wait()
    for slot in range(4):
        if slot or not at_lo:
            settle(slot)
        if slot:
            beside_y(slot)
    if at_lo:
        edge(at_x > 0, 0, 1)

    def forward(t):
        for row in (t, t + 1):
            p_copy(row).wait()
        for row in (t, t + 1):
            dot_y(jnp.maximum(row - 4, 0))
        for row in (t, t + 1):
            dot_z(jnp.maximum(row - 2, 0))
        for row in (t, t + 1):
            advance(row)

    def step(n, carry):
        t = 2 * n
        for slot in (t + 4, t + 5):
            s_copy(slot - 1).wait()
            m_copy(slot).wait()
        forward(t)
        for slot in (t + 4, t + 5):
            settle(slot)
            beside_y(slot)
        for row in (t, t + 1):
            a_copy(row).start()
        return carry

    lax.fori_loop(0, rows // 2 - 2, step, 0)
    s_copy(rows - 1).wait()
    m_copy(rows).wait()
    if not at_hi:
        m_copy(rows + 1).wait()
    forward(rows - 4)
    settle(rows)
    beside_y(rows)
    if at_hi:
        edge(at_x < peers[0] - 1, rows + 1, rows)
    else:
        settle(rows + 1)
    for row in (rows - 4, rows - 3):
        a_copy(row).start()
    last = (rows - 2, rows - 1)
    forward(rows - 2)
    for row in last:
        a_copy(row).start()
    for row in last:
        dot_y(row - 2)
    for row in last:
        dot_z(row)
    for row in last:
        dot_y(row)

    def finish(row, carry):
        a_copy(row).wait()
        return carry

    lax.fori_loop(0, rows, finish, 0)
    for copy in x_copies:
        copy.wait()


def second_stage(first_row, rows, middle, scalar, prefactor, y_lo, y_hi, factor_z, mix, beside, previous, after, sends):
    _, cells_y, depth = scalar.shape
    ranks, z_rank = mix.shape[0], factor_z.shape[1]
    tiles, cells = depth // lanes, rows * cells_y * depth
    part = jax.ShapeDtypeStruct((rows, ranks // 2, z_rank), f32)
    messages = [jax.ShapeDtypeStruct((tiles, 2 * cells_y + pad, lanes), f32)] * (2 * sends)
    operands = [middle, scalar, prefactor, y_lo, y_hi, factor_z, mix, *beside]
    specs = [in_hbm] * (7 + len(beside))
    aliases = {}
    if previous is not None:
        aliases = {len(operands): 0}
        operands.append(previous)
        specs.append(in_hbm)
    operands += after
    specs += [in_hbm] * len(after)
    return pl.pallas_call(
        functools.partial(
            second_kernel, first_row, rows, len(beside), sends, (lax.axis_size("gx"), lax.axis_size("gy"))
        ),
        out_shape=(jax.ShapeDtypeStruct(scalar.shape, f32), part, part, *messages),
        in_specs=specs,
        out_specs=[in_hbm] + [in_vmem] * (2 + len(messages)),
        input_output_aliases=aliases,
        scratch_shapes=[
            pltpu.VMEM((tiles, rows + 2, cells_y + 2 * pad, lanes), f32),
            pltpu.VMEM((rows + 1, cells_y, depth), f32),
            pltpu.VMEM((rows, cells_y, depth), f32),
            pltpu.VMEM((rows, cells_y, depth), f32),
            pltpu.VMEM((rows, cells_y, depth), bf16),
            pltpu.VMEM((rows, cells_y, z_rank), f32),
            pltpu.VMEM(y_lo.shape, f32),
            pltpu.VMEM(y_hi.shape, f32),
            pltpu.VMEM(factor_z.shape, factor_z.dtype),
            pltpu.VMEM(mix.shape, bf16),
            pltpu.VMEM((tiles, 2 * cells_y + pad, lanes), f32),
            pltpu.SemaphoreType.DMA((rows + 2,)),
            pltpu.SemaphoreType.DMA((rows,)),
            pltpu.SemaphoreType.DMA((rows,)),
            pltpu.SemaphoreType.DMA((rows,)),
            pltpu.SemaphoreType.DMA((2, tiles + 1)),
            pltpu.SemaphoreType.DMA((5,)),
        ],
        cost_estimate=pl.CostEstimate(
            flops=30 * cells + 2 * cells * z_rank, bytes_accessed=16 * cells, transcendentals=2 * cells
        ),
        compiler_params=room,
    )(*operands)


def shift(array, axis, step):
    peers = lax.axis_size(axis)
    return lax.ppermute(array, axis, [(i, i + step) for i in range(peers) if 0 <= i + step < peers])


def swap(array, axis, distance):
    return lax.ppermute(array, axis, [(i, i ^ distance) for i in range(lax.axis_size(axis))])


def gathered(array, axis):
    peers = lax.axis_size(axis)
    me, distance, place = lax.axis_index(axis), peers // 2, 0
    while distance:
        other = swap(array, axis, distance)
        upper = (me & distance) != 0
        array = jnp.stack([jnp.where(upper, other, array), jnp.where(upper, array, other)], axis=place)
        distance, place = distance // 2, place + 1
    return array.reshape((-1,) + array.shape[-1:])


def runs_of(cells_x):
    part = cells_x // 16
    return [(2 * part, 9 * part), (11 * part, 5 * part), (0, 2 * part)]


def on_device(scalar, prefactor, factor_x, factor_y, factor_z):
    cells_x, _, _ = scalar.shape
    peers_x, peers_y = lax.axis_size("gx"), lax.axis_size("gy")
    y_rank, z_rank = factor_y.shape[1], factor_z.shape[1]
    block = y_rank // peers_y

    to_y_lo, to_y_hi, mix = faces(scalar, prefactor, factor_y)
    y_lo, y_hi = shift(to_y_hi, "gy", 1), shift(to_y_lo, "gy", -1)
    middle = first_stage(scalar, prefactor, to_y_lo)

    def halved(run):
        number, held, coming, distance = run
        held = held + coming
        if 2 * distance == peers_y:
            owned[number] = held
            return []
        half = held.shape[1] // 2
        coming = swap(held[:, half:], "gy", 2 * distance)
        return [(number, held[:, :half], coming, 2 * distance)]

    all_x = gathered(factor_x, "gx")
    runs = runs_of(cells_x)
    advanced, owned, in_flight = None, {}, []
    for number, (first_row, rows) in enumerate(runs):
        beside = [x_lo] * (first_row == 0) + [x_hi] * (first_row + rows == cells_x) if number else []
        advanced, keep, send, *messages = second_stage(
            first_row, rows, middle, scalar, prefactor, y_lo, y_hi, factor_z, mix, beside, advanced, [], not number
        )
        in_flight = sum((halved(run) for run in in_flight), [])
        in_flight.append((number, keep, swap(send, "gy", 1), 1))
        if messages:
            x_lo = shift(messages[1], "gx", 1)
            x_hi = shift(messages[0], "gx", -1)
    while in_flight:
        in_flight = sum((halved(run) for run in in_flight), [])
    owned = jnp.concatenate([owned[number] for number in sorted(owned, key=lambda n: runs[n][0])], axis=0)

    columns = block * z_rank // peers_x
    parts = owned.reshape(cells_x, peers_x, columns).transpose(1, 0, 2)
    parts = lax.all_to_all(parts, "gx", 0, 0, tiled=True).reshape(peers_x * cells_x, columns)
    core = jnp.einsum("xa,xn->an", all_x, parts, precision=lax.Precision.HIGHEST)
    core = core.reshape(peers_x, -1, columns)
    core = lax.all_to_all(core, "gx", 0, 0, tiled=True)
    core = core.transpose(1, 0, 2).reshape(-1, block, z_rank)
    return (advanced, core)


def solution(mesh):
    return jax.shard_map(
        on_device,
        mesh=mesh,
        in_specs=(P("gx", "gy", None), P("gx", "gy", None), P("gx", None), P("gy", None), P()),
        out_specs=(P("gx", "gy", None), P("gx", "gy", None)),
        check_vma=False,
    )
```

```python
import functools
import math

import jax
import jax.numpy as jnp
from jax import lax
from jax.experimental import pallas as pl
from jax.experimental.pallas import tpu as pltpu
from jax.sharding import PartitionSpec as P

spread_rate = 0.12
kept_rate = 1.0 - 6.0 * spread_rate
activation = 2.0
exponent = -activation * math.log2(math.e)
lanes = 128
piece = 32
pad = 8
group = 8
f32, bf16 = jnp.float32, jnp.bfloat16
room = pltpu.CompilerParams(vmem_limit_bytes=58 << 20)
in_hbm = pl.BlockSpec(memory_space=pltpu.HBM)
in_vmem = pl.BlockSpec(memory_space=pltpu.VMEM)


def source(field, prefactor):
    return prefactor * jnp.exp2(exponent / (1.0 + field * field))


def along_z(tiles):
    lane = lax.broadcasted_iota(jnp.int32, tiles[0].shape, 1)
    last = len(tiles) - 1
    sums = []
    for k, tile in enumerate(tiles):
        below = tiles[k - 1] if k else 0.0
        above = tiles[k + 1] if k < last else 0.0
        left = pltpu.roll(jnp.where(lane == lanes - 1, below, tile), 1, 1)
        right = pltpu.roll(jnp.where(lane == 0, above, tile), lanes - 1, 1)
        sums.append(left + right)
    return sums


def column(k):
    return slice(k * lanes, (k + 1) * lanes)


def beside_z(tile, below, above):
    lane = lax.broadcasted_iota(jnp.int32, tile.shape, 1)
    left = pltpu.roll(jnp.where(lane == lanes - 1, below, tile), 1, 1)
    right = pltpu.roll(jnp.where(lane == 0, above, tile), lanes - 1, 1)
    return left + right


def neighbours(buf, slot, k, first, count):
    def cells(k, slot, y):
        return buf[k, slot, pl.ds(pad + y, count), :]

    own = cells(k, slot, first)
    below = cells(k - 1, slot, first) if k else 0.0
    above = cells(k + 1, slot, first) if k < buf.shape[0] - 1 else 0.0
    beside = (cells(k, slot - 1, first) + cells(k, slot + 1, first)) + (
        cells(k, slot, first - 1) + cells(k, slot, first + 1)
    )
    return own, beside + beside_z(own, below, above)


def faces_kernel(peers_y, scalar, prefactor, factor_y, y_lo, y_hi, mix, s_cols, p_cols, line, turned, sems):
    cells_x, cells_y, depth = scalar.shape
    tiles = depth // lanes

    def copies_of(n, source, first_y, buf, side):
        return [
            pltpu.make_async_copy(
                source.at[:, pl.ds(first_y, 8), pl.ds(k * lanes, lanes)],
                buf.at[side, k].reshape(cells_x, 8, lanes),
                sems.at[n, k],
            )
            for k in range(tiles)
        ]

    copies = [
        copies_of(0, scalar, 0, s_cols, 0),
        copies_of(1, prefactor, 0, p_cols, 0),
        copies_of(2, scalar, cells_y - 8, s_cols, 1),
        copies_of(3, prefactor, cells_y - 8, p_cols, 1),
    ]
    for some in copies:
        for one in some:
            one.start()

    ranks = factor_y.shape[1]
    block = ranks // peers_y
    turned[...] = factor_y[...].T
    at_y = lax.axis_index("gy")
    bits = peers_y.bit_length() - 1
    for n in range(peers_y):
        other = int(format(n, f"0{bits}b")[::-1], 2) if bits else 0
        rows = turned[pl.ds(pl.multiple_of((at_y ^ other) * block, block), block), :]
        high = rows.astype(bf16)
        low = (rows - high.astype(f32)).astype(bf16)
        mix[n * block : (n + 1) * block, :] = jnp.concatenate([high, high, low], axis=1)

    for k in range(tiles):
        line[k, 0:pad, :] = jnp.zeros((pad, lanes), f32)
        line[k, pad + cells_x :, :] = jnp.zeros((pad, lanes), f32)
    for side, (out, edge, next_in) in enumerate(((y_lo, 0, 1), (y_hi, 7, 6))):
        for one in copies[2 * side] + copies[2 * side + 1]:
            one.wait()

        def cells(buf, y, k):
            return buf[side, k, pl.ds(y, cells_x, stride=8), :]

        own = [cells(s_cols, edge, k) for k in range(tiles)]
        for k in range(tiles):
            line[k, pad : pad + cells_x, :] = own[k]
        for k, z_sum in enumerate(along_z(own)):
            beside = line[k, pad - 1 : pad - 1 + cells_x, :] + line[k, pad + 1 : pad + 1 + cells_x, :]
            beside = beside + z_sum + cells(s_cols, next_in, k)
            out[0, k] = spread_rate * own[k]
            out[1, k] = spread_rate * beside + (kept_rate * own[k] + source(own[k], cells(p_cols, edge, k)))


def faces(scalar, prefactor, factor_y):
    cells_x, cells_y, depth = scalar.shape
    ranks = factor_y.shape[1]
    face = jax.ShapeDtypeStruct((2, depth // lanes, cells_x, lanes), f32)
    factors = jax.ShapeDtypeStruct((ranks, 3 * cells_y), bf16)
    return pl.pallas_call(
        functools.partial(faces_kernel, lax.axis_size("gy")),
        out_shape=(face, face, factors),
        in_specs=[in_hbm, in_hbm, in_vmem],
        out_specs=[in_vmem] * 3,
        scratch_shapes=[
            pltpu.VMEM((2, depth // lanes, cells_x * 8, lanes), f32),
            pltpu.VMEM((2, depth // lanes, cells_x * 8, lanes), f32),
            pltpu.VMEM((depth // lanes, cells_x + 2 * pad, lanes), f32),
            pltpu.VMEM((ranks, cells_y), f32),
            pltpu.SemaphoreType.DMA((4, depth // lanes)),
        ],
        compiler_params=room,
        name="faces",
    )(scalar, prefactor, factor_y)


def first_kernel(scalar, prefactor, after, middle, s_buf, p_buf, m_buf, s_sem, p_sem, m_sem):
    cells_x, cells_y, depth = scalar.shape
    tiles = depth // lanes
    groups = cells_x // group

    def s_copy(g, k):
        return pltpu.make_async_copy(
            scalar.at[pl.ds(g * group, group), :, pl.ds(k * lanes, lanes)],
            s_buf.at[k, pl.ds(g * group + 1, group), pl.ds(pad, cells_y)],
            s_sem.at[g, k],
        )

    def p_copy(g):
        rows = pl.ds(g * group, group)
        return pltpu.make_async_copy(prefactor.at[rows], p_buf.at[rows], p_sem.at[g])

    def m_copy(g):
        rows = pl.ds(g * group, group)
        return pltpu.make_async_copy(m_buf.at[:, rows], middle.at[:, rows], m_sem.at[g])

    def start(g, carry):
        for k in range(tiles):
            s_copy(g, k).start()
        p_copy(g).start()
        return carry

    lax.fori_loop(0, groups, start, 0)

    for k in range(tiles):
        s_buf[k, 0, pad : pad + cells_y, :] = jnp.zeros((cells_y, lanes), f32)
        s_buf[k, cells_x + 1, pad : pad + cells_y, :] = jnp.zeros((cells_y, lanes), f32)

    def clear(row, carry):
        for k in range(tiles):
            s_buf[k, row + 1, 0:pad, :] = jnp.zeros((pad, lanes), f32)
            s_buf[k, row + 1, pad + cells_y :, :] = jnp.zeros((pad, lanes), f32)
        return carry

    lax.fori_loop(0, cells_x, clear, 0)

    def wait_s(g):
        for k in range(tiles):
            s_copy(g, k).wait()

    pieces = [(k, y) for k in range(tiles) for y in range(0, cells_y, piece)]

    def row_of(row):
        for k, y in pieces:
            own, beside = neighbours(s_buf, row + 1, k, y, piece)
            m_buf[k, row, pl.ds(y, piece), :] = spread_rate * beside + (
                kept_rate * own + source(own, p_buf[row, pl.ds(y, piece), column(k)])
            )

    def rows_of(g):
        p_copy(g).wait()

        def one(r, carry):
            row_of(g * group + r)
            return carry

        lax.fori_loop(0, group, one, 0, unroll=True)
        m_copy(g).start()

    wait_s(0)

    def step(g, carry):
        wait_s(g + 1)
        rows_of(g)
        return carry

    lax.fori_loop(0, groups - 1, step, 0)
    rows_of(groups - 1)

    def finish(g, carry):
        m_copy(g).wait()
        return carry

    lax.fori_loop(0, groups, finish, 0)


def first_stage(scalar, prefactor, after):
    cells_x, cells_y, depth = scalar.shape
    tiles, cells = depth // lanes, math.prod(scalar.shape)
    groups = cells_x // group
    return pl.pallas_call(
        first_kernel,
        out_shape=jax.ShapeDtypeStruct((tiles, cells_x, cells_y, lanes), f32),
        in_specs=[in_hbm] * 3,
        out_specs=in_hbm,
        scratch_shapes=[
            pltpu.VMEM((tiles, cells_x + 2, cells_y + 2 * pad, lanes), f32),
            pltpu.VMEM((cells_x, cells_y, depth), f32),
            pltpu.VMEM((tiles, cells_x, cells_y, lanes), f32),
            pltpu.SemaphoreType.DMA((groups, tiles)),
            pltpu.SemaphoreType.DMA((groups,)),
            pltpu.SemaphoreType.DMA((groups,)),
        ],
        cost_estimate=pl.CostEstimate(flops=24 * cells, bytes_accessed=12 * cells, transcendentals=2 * cells),
        compiler_params=room,
        name="first_stage",
    )(scalar, prefactor, after)


def second_kernel(first_row, rows, n_extra, sends, peers, middle, scalar, prefactor, y_lo_in, y_hi_in, factor_z_in, mix_in, *rest):
    (m_buf, s_buf, p_buf, a_buf, low_buf, z_buf, y_lo, y_hi, factor_z, mix, face, m_sem, s_sem, p_sem, a_sem, x_sem, y_sem) = rest[-17:]
    messages = rest[-19:-17] if sends else ()
    (advanced, keep, send) = rest[-22:-19] if sends else rest[-20:-17]
    cells_x, cells_y, depth = scalar.shape
    tiles = depth // lanes
    at_lo, at_hi = first_row == 0, first_row + rows == cells_x
    end = pad + cells_y
    half = keep.shape[1]
    at_x, at_y = lax.axis_index("gx"), lax.axis_index("gy")

    def share(there):
        return jnp.where(there, spread_rate, 0.0).astype(f32)

    y_shares = (share(at_y > 0), share(at_y < peers[1] - 1))

    def m_copy(slot):
        return pltpu.make_async_copy(
            middle.at[:, first_row - 1 + slot], m_buf.at[:, slot, pl.ds(pad, cells_y)], m_sem.at[slot]
        )

    def s_copy(row):
        return pltpu.make_async_copy(scalar.at[first_row + row], s_buf.at[row], s_sem.at[row])

    def p_copy(row):
        return pltpu.make_async_copy(prefactor.at[first_row + row], p_buf.at[row], p_sem.at[row])

    def a_copy(row):
        return pltpu.make_async_copy(a_buf.at[row], advanced.at[first_row + row], a_sem.at[row])

    def start(row, carry):
        m_copy(row + 1).start()
        s_copy(row).start()
        p_copy(row).start()
        return carry

    small = [(y_lo_in, y_lo), (y_hi_in, y_hi), (factor_z_in, factor_z), (mix_in, mix)]
    small += [(rest[0], face)] * n_extra
    small = [pltpu.make_async_copy(a, b, y_sem.at[n]) for n, (a, b) in enumerate(small)]
    if not at_lo:
        m_copy(0).start()
    for row in range(3):
        start(row, 0)
    for copy in small:
        copy.start()
    lax.fori_loop(3, rows, start, 0)
    if not at_hi:
        m_copy(rows + 1).start()

    for copy in small:
        copy.wait()

    x_copies = []
    for n, message in enumerate(messages):
        row = n * (cells_x - 1)
        for k in range(tiles):
            x_copies.append(
                pltpu.make_async_copy(
                    scalar.at[row, :, pl.ds(k * lanes, lanes)], message.at[k, pl.ds(0, cells_y)], x_sem.at[n, k]
                )
            )
            message[k, 2 * cells_y : 2 * cells_y + 1, :] = y_lo[0, k, row : row + 1, :]
            message[k, 2 * cells_y + 1 : 2 * cells_y + 2, :] = y_hi[0, k, row : row + 1, :]
        x_copies.append(
            pltpu.make_async_copy(
                middle.at[:, row], message.at[:, pl.ds(cells_y, cells_y)], x_sem.at[n, tiles]
            )
        )
    for copy in x_copies:
        copy.start()

    def add(k, slot, y, value):
        m_buf[k, slot, pl.ds(y, 1), :] = m_buf[k, slot, pl.ds(y, 1), :] + value

    def settle(slot):
        row = first_row - 1 + slot
        for k in range(tiles):
            add(k, slot, pad, y_lo[0, k, pl.ds(row, 1), :])
            add(k, slot, end - 1, y_hi[0, k, pl.ds(row, 1), :])

    def beside_y(slot):
        row = first_row - 1 + slot
        for k in range(tiles):
            m_buf[k, slot, pad - 1 : pad, :] = (
                y_lo[1, k, pl.ds(row, 1), :] + y_shares[0] * s_buf[slot - 1, 0:1, column(k)]
            )
            m_buf[k, slot, end : end + 1, :] = (
                y_hi[1, k, pl.ds(row, 1), :] + y_shares[1] * s_buf[slot - 1, cells_y - 1 : cells_y, column(k)]
            )

    def edge(there, slot, own_slot):
        part = share(there)
        for k in range(tiles):
            m_buf[k, slot, pad:end, :] = face[k, cells_y : 2 * cells_y, :] + part * s_buf[own_slot - 1, :, column(k)]
            m_buf[k, own_slot, pad:end, :] = m_buf[k, own_slot, pad:end, :] + spread_rate * face[k, :cells_y, :]
            below, above = face[k, 2 * cells_y : 2 * cells_y + 1, :], face[k, 2 * cells_y + 1 : 2 * cells_y + 2, :]
            add(k, slot, pad, below)
            add(k, slot, end - 1, above)
            add(k, own_slot, pad - 1, below)
            add(k, own_slot, end, above)

    def dot_z(row):
        z_buf[row] = jnp.dot(low_buf[row], factor_z[...], preferred_element_type=f32)

    def dot_y(row):
        z = z_buf[row]
        high = z.astype(bf16)
        low = (z - high.astype(f32)).astype(bf16)
        y = jnp.dot(mix[...], jnp.concatenate([high, low, high], axis=0), preferred_element_type=f32)
        keep[row] = y[:half]
        send[row] = y[half:]

    pieces = [(k, y) for k in range(tiles) for y in range(0, cells_y, piece)]

    def advance(row):
        slot = row + 1
        for k, y in pieces:
            own, beside = neighbours(m_buf, slot, k, y, piece)
            value = source(own, p_buf[row, pl.ds(y, piece), column(k)]) + s_buf[row, pl.ds(y, piece), column(k)]
            value = 0.5 * (value + (spread_rate * beside + kept_rate * own))
            a_buf[row, pl.ds(y, piece), column(k)] = value
            low_buf[row, pl.ds(y, piece), column(k)] = value.astype(bf16)

    for slot in range(4):
        if slot or not at_lo:
            m_copy(slot).wait()
    for row in range(3):
        s_copy(row).wait()
    for slot in range(4):
        if slot or not at_lo:
            settle(slot)
        if slot:
            beside_y(slot)
    if at_lo:
        edge(at_x > 0, 0, 1)

    def forward(t):
        for row in (t, t + 1):
            p_copy(row).wait()
        for row in (t, t + 1):
            dot_y(jnp.maximum(row - 4, 0))
        for row in (t, t + 1):
            dot_z(jnp.maximum(row - 2, 0))
        for row in (t, t + 1):
            advance(row)

    def step(n, carry):
        t = 2 * n
        for slot in (t + 4, t + 5):
            s_copy(slot - 1).wait()
            m_copy(slot).wait()
        forward(t)
        for slot in (t + 4, t + 5):
            settle(slot)
            beside_y(slot)
        for row in (t, t + 1):
            a_copy(row).start()
        return carry

    lax.fori_loop(0, rows // 2 - 2, step, 0)
    s_copy(rows - 1).wait()
    m_copy(rows).wait()
    if not at_hi:
        m_copy(rows + 1).wait()
    forward(rows - 4)
    settle(rows)
    beside_y(rows)
    if at_hi:
        edge(at_x < peers[0] - 1, rows + 1, rows)
    else:
        settle(rows + 1)
    for row in (rows - 4, rows - 3):
        a_copy(row).start()
    last = (rows - 2, rows - 1)
    forward(rows - 2)
    for row in last:
        a_copy(row).start()
    for row in last:
        dot_y(row - 2)
    for row in last:
        dot_z(row)
    for row in last:
        dot_y(row)

    def finish(row, carry):
        a_copy(row).wait()
        return carry

    lax.fori_loop(0, rows, finish, 0)
    for copy in x_copies:
        copy.wait()


def second_stage(first_row, rows, middle, scalar, prefactor, y_lo, y_hi, factor_z, mix, beside, previous, after, sends):
    _, cells_y, depth = scalar.shape
    ranks, z_rank = mix.shape[0], factor_z.shape[1]
    tiles, cells = depth // lanes, rows * cells_y * depth
    part = jax.ShapeDtypeStruct((rows, ranks // 2, z_rank), f32)
    messages = [jax.ShapeDtypeStruct((tiles, 2 * cells_y + pad, lanes), f32)] * (2 * sends)
    operands = [middle, scalar, prefactor, y_lo, y_hi, factor_z, mix, *beside]
    specs = [in_hbm] * (7 + len(beside))
    aliases = {}
    if previous is not None:
        aliases = {len(operands): 0}
        operands.append(previous)
        specs.append(in_hbm)
    operands += after
    specs += [in_hbm] * len(after)
    return pl.pallas_call(
        functools.partial(
            second_kernel, first_row, rows, len(beside), sends, (lax.axis_size("gx"), lax.axis_size("gy"))
        ),
        out_shape=(jax.ShapeDtypeStruct(scalar.shape, f32), part, part, *messages),
        in_specs=specs,
        out_specs=[in_hbm] + [in_vmem] * (2 + len(messages)),
        input_output_aliases=aliases,
        scratch_shapes=[
            pltpu.VMEM((tiles, rows + 2, cells_y + 2 * pad, lanes), f32),
            pltpu.VMEM((rows + 1, cells_y, depth), f32),
            pltpu.VMEM((rows, cells_y, depth), f32),
            pltpu.VMEM((rows, cells_y, depth), f32),
            pltpu.VMEM((rows, cells_y, depth), bf16),
            pltpu.VMEM((rows, cells_y, z_rank), f32),
            pltpu.VMEM(y_lo.shape, f32),
            pltpu.VMEM(y_hi.shape, f32),
            pltpu.VMEM(factor_z.shape, factor_z.dtype),
            pltpu.VMEM(mix.shape, bf16),
            pltpu.VMEM((tiles, 2 * cells_y + pad, lanes), f32),
            pltpu.SemaphoreType.DMA((rows + 2,)),
            pltpu.SemaphoreType.DMA((rows,)),
            pltpu.SemaphoreType.DMA((rows,)),
            pltpu.SemaphoreType.DMA((rows,)),
            pltpu.SemaphoreType.DMA((2, tiles + 1)),
            pltpu.SemaphoreType.DMA((5,)),
        ],
        cost_estimate=pl.CostEstimate(
            flops=30 * cells + 2 * cells * z_rank, bytes_accessed=16 * cells, transcendentals=2 * cells
        ),
        compiler_params=room,
    )(*operands)


def shift(array, axis, step):
    peers = lax.axis_size(axis)
    return lax.ppermute(array, axis, [(i, i + step) for i in range(peers) if 0 <= i + step < peers])


def swap(array, axis, distance):
    return lax.ppermute(array, axis, [(i, i ^ distance) for i in range(lax.axis_size(axis))])


def gathered(array, axis):
    peers = lax.axis_size(axis)
    me, distance, place = lax.axis_index(axis), peers // 2, 0
    while distance:
        other = swap(array, axis, distance)
        upper = (me & distance) != 0
        array = jnp.stack([jnp.where(upper, other, array), jnp.where(upper, array, other)], axis=place)
        distance, place = distance // 2, place + 1
    return array.reshape((-1,) + array.shape[-1:])


def runs_of(cells_x):
    part = cells_x // 16
    return [(2 * part, 9 * part), (11 * part, 5 * part), (0, 2 * part)]


def on_device(scalar, prefactor, factor_x, factor_y, factor_z):
    cells_x, _, _ = scalar.shape
    peers_x, peers_y = lax.axis_size("gx"), lax.axis_size("gy")
    y_rank, z_rank = factor_y.shape[1], factor_z.shape[1]
    block = y_rank // peers_y

    to_y_lo, to_y_hi, mix = faces(scalar, prefactor, factor_y)
    y_lo, y_hi = shift(to_y_hi, "gy", 1), shift(to_y_lo, "gy", -1)
    middle = first_stage(scalar, prefactor, to_y_lo)

    def halved(run):
        number, held, coming, distance = run
        held = held + coming
        if 2 * distance == peers_y:
            owned[number] = held
            return []
        half = held.shape[1] // 2
        coming = swap(held[:, half:], "gy", 2 * distance)
        return [(number, held[:, :half], coming, 2 * distance)]

    all_x = gathered(factor_x, "gx")
    runs = runs_of(cells_x)
    advanced, owned, in_flight = None, {}, []
    for number, (first_row, rows) in enumerate(runs):
        beside = [x_lo] * (first_row == 0) + [x_hi] * (first_row + rows == cells_x) if number else []
        advanced, keep, send, *messages = second_stage(
            first_row, rows, middle, scalar, prefactor, y_lo, y_hi, factor_z, mix, beside, advanced, [], not number
        )
        in_flight = sum((halved(run) for run in in_flight), [])
        in_flight.append((number, keep, swap(send, "gy", 1), 1))
        if messages:
            x_lo = shift(messages[1], "gx", 1)
            x_hi = shift(messages[0], "gx", -1)
    while in_flight:
        in_flight = sum((halved(run) for run in in_flight), [])
    columns = block * z_rank // peers_x
    parts = [owned[n].reshape(-1, peers_x, columns).transpose(1, 0, 2) for n in sorted(owned, key=lambda n: runs[n][0])]
    parts = jnp.concatenate(parts, axis=1)
    parts = lax.all_to_all(parts, "gx", 0, 0, tiled=True).reshape(peers_x * cells_x, columns)
    core = jnp.einsum("xa,xn->an", all_x, parts, precision=lax.Precision.HIGH)
    core = core.reshape(peers_x, -1, columns)
    core = lax.all_to_all(core, "gx", 0, 0, tiled=True)
    core = core.transpose(1, 0, 2).reshape(-1, block, z_rank)
    return (advanced, core)


def solution(mesh):
    return jax.shard_map(
        on_device,
        mesh=mesh,
        in_specs=(P("gx", "gy", None), P("gx", "gy", None), P("gx", None), P("gy", None), P()),
        out_specs=(P("gx", "gy", None), P("gx", "gy", None)),
        check_vma=False,
    )
```
